256 devices in a mesh: lat: 16 (over x_lo, y, core), lon: 16 (over z, x_hi).
Axes of the slice: x: 4 (x_hi: 2, x_lo: 2; x = x_hi * 2 + x_lo), y: 4, z: 8, core: 2. Of those that a mesh axis runs over, the one named last changes fastest.
Arguments:
- current_sample: float32 [4, 512, 4096], P(None, 'lat', 'lon'), may hold values from -6 to 6
- churn_noise: float32 [4, 512, 4096], P(None, 'lat', 'lon'), may hold values from -6 to 6
- coarse_fields: float32 [12, 64, 512], P(None, 'lat', 'lon'), may hold values from -6 to 6
- tile_owner: int32 [16], replicated, may hold values from 0 to 15, each once
- input_kernel: bfloat16 [3, 3, 16, 128], replicated, may hold values from -0.5 to 0.5
- fine_first: bfloat16 [3, 3, 128, 128], replicated, may hold values from -0.1875 to 0.1875
- fine_second: bfloat16 [3, 3, 128, 128], replicated, may hold values from -0.1875 to 0.1875
- coarse_first: bfloat16 [3, 3, 128, 128], replicated, may hold values from -0.1875 to 0.1875
- coarse_second: bfloat16 [3, 3, 128, 128], replicated, may hold values from -0.1875 to 0.1875
- output_kernel: bfloat16 [3, 3, 128, 4], replicated, may hold values from -0.5 to 0.5
Outputs:
- next_sample: float32 [4, 512, 4096], P(None, 'lat', 'lon')
The draws below stay inside these ranges and needn't reach their ends.
Inputs may be any that keep to these rules, and one draw needn't show every extreme that they name: `tile_owner`: each value is the row block's position along the bands; every stored block covers exactly one band.
All inputs are finite; a program needn't handle non-finite values.
Results may differ from the reference program's by a relative error of at most 0.0055.
Values may be sent and summed in bfloat16 or wider, within the bound.
No kernel may reach another device: no remote copies, remote signals or barrier semaphores. Data moves between devices by JAX's collectives and lax.ppermute only.
A program may use at most 64 MiB of HBM per device.

```python
import math
import jax
import jax.numpy as jnp
from jax import lax

CH = 128
VARS = 4
CVARS = 12
RATIO = 8
NLAT = 512
NLON = 4096
BANDS = 16


def block_levels(key, extent, split, smallest, largest):
    def one(position, blocks):
        draws = jax.random.uniform(jax.random.fold_in(jax.random.fold_in(key, 6), position), (blocks,), jnp.float32, smallest / len(split), largest / len(split))
        return jnp.repeat(jnp.exp(draws), extent[position] // blocks).reshape((-1,) + (1,) * (len(extent) - position - 1))

    level = one(*split[0])
    for cut in split[1:]:
        level = level * one(*cut)
    return level


def centred(stream_key, dims, spread, most, split=(), held_as=jnp.bfloat16):
    array = spread * jax.random.normal(stream_key, dims, jnp.float32)
    if split:
        array = array * block_levels(stream_key, dims, split, -0.22, 0.18)
    return jnp.clip(array, -most, most).astype(held_as)


def setup_inputs(seed: int = 0) -> dict:
    streams_of = jax.random.split(jax.random.key(seed), 11)
    current_sample = centred(streams_of[0], (VARS, NLAT, NLON), 1.0, 6.0, ((1, 16), (2, 16)), jnp.float32)
    churn_noise = centred(streams_of[1], (VARS, NLAT, NLON), 1.0, 6.0, ((1, 16), (2, 16)), jnp.float32)
    coarse_fields = centred(streams_of[2], (CVARS, NLAT // RATIO, NLON // RATIO), 1.0, 6.0, ((1, 16), (2, 16)), jnp.float32)
    tile_owner = jax.random.permutation(streams_of[3], BANDS).astype(jnp.int32)
    input_kernel = centred(streams_of[4], (3, 3, VARS + CVARS, CH), (9 * (VARS + CVARS)) ** -0.5, 0.5)
    fine_first = centred(streams_of[5], (3, 3, CH, CH), (9 * CH) ** -0.5, 0.1875)
    fine_second = centred(streams_of[6], (3, 3, CH, CH), (9 * CH) ** -0.5, 0.1875)
    coarse_first = centred(streams_of[7], (3, 3, CH, CH), (9 * CH) ** -0.5, 0.1875)
    coarse_second = centred(streams_of[8], (3, 3, CH, CH), (9 * CH) ** -0.5, 0.1875)
    output_kernel = centred(streams_of[9], (3, 3, CH, VARS), CH ** -0.5, 0.5)
    return {"current_sample": current_sample, "churn_noise": churn_noise, "coarse_fields": coarse_fields, "tile_owner": tile_owner, "input_kernel": input_kernel, "fine_first": fine_first, "fine_second": fine_second, "coarse_first": coarse_first, "coarse_second": coarse_second, "output_kernel": output_kernel}


sigma_now = 1.0
sigma_hat = 1.2
sigma_next = 0.4
sigma_data = 0.5

def sphere_pad(values):
    half = values.shape[2] // 2
    north_rows = jnp.roll(values[:, :1, :], -half, axis=2)
    south_rows = jnp.roll(values[:, -1:, :], -half, axis=2)
    with_rows = jnp.concatenate([north_rows, values, south_rows], axis=1)
    return jnp.concatenate([with_rows[:, :, -1:], with_rows, with_rows[:, :, :1]], axis=2)

def convolve(values, kernel):
    padded = sphere_pad(values).astype(jnp.float32)[None]
    result = lax.conv_general_dilated(padded, kernel.astype(jnp.float32), (1, 1), 'VALID', dimension_numbers=('NCHW', 'HWIO', 'NCHW'), precision=lax.Precision.HIGHEST)
    return result[0]

def silu_round(values):
    return jax.nn.silu(values.astype(jnp.float32)).astype(jnp.bfloat16)

def reference(current_sample, churn_noise, coarse_fields, tile_owner, input_kernel, fine_first, fine_second, coarse_first, coarse_second, output_kernel):
    band_count = tile_owner.shape[0]
    block_rows = coarse_fields.shape[1] // band_count
    blocks = coarse_fields.reshape(coarse_fields.shape[0], band_count, block_rows, coarse_fields.shape[2])
    condition = jnp.take(blocks, tile_owner, axis=1).reshape(coarse_fields.shape)
    condition = jnp.repeat(jnp.repeat(condition, RATIO, axis=1), RATIO, axis=2)
    perturbed = current_sample + math.sqrt(sigma_hat ** 2 - sigma_now ** 2) * churn_noise
    scale_in = 1.0 / math.sqrt(sigma_hat ** 2 + sigma_data ** 2)
    net_in = jnp.concatenate([perturbed * scale_in, condition], axis=0).astype(jnp.bfloat16)
    stem = convolve(net_in, input_kernel).astype(jnp.bfloat16)
    fine_act = silu_round(stem)
    fine_hidden = silu_round(convolve(fine_act, fine_first))
    fine_out = ((stem.astype(jnp.float32) + convolve(fine_hidden, fine_second)) * math.sqrt(0.5)).astype(jnp.bfloat16)
    channels, lat_rows, lon_cols = fine_out.shape
    pooled = fine_out.astype(jnp.float32).reshape(channels, lat_rows // 2, 2, lon_cols // 2, 2).mean(axis=(2, 4)).astype(jnp.bfloat16)
    coarse_act = silu_round(pooled)
    coarse_hidden = silu_round(convolve(coarse_act, coarse_first))
    coarse_out = ((pooled.astype(jnp.float32) + convolve(coarse_hidden, coarse_second)) * math.sqrt(0.5)).astype(jnp.bfloat16)
    widened = jnp.repeat(jnp.repeat(coarse_out, 2, axis=1), 2, axis=2)
    merged = silu_round((fine_out.astype(jnp.float32) + widened.astype(jnp.float32)) * math.sqrt(0.5))
    network = convolve(merged, output_kernel)
    denom = sigma_hat ** 2 + sigma_data ** 2
    denoised = sigma_data ** 2 / denom * perturbed + sigma_hat * sigma_data / math.sqrt(denom) * network
    return perturbed + (sigma_next - sigma_hat) / sigma_hat * (perturbed - denoised)
```

```python
import math

import jax
import jax.numpy as jnp
from jax import lax
from jax.experimental import pallas as pl
from jax.experimental.pallas import tpu as pltpu
from jax.sharding import PartitionSpec as P

RATIO = 8
CH = 128
ROWS = 32
COLS = 256
ROW_HALO = 9
COL_HALO = 16
EXT_ROWS = ROWS + 2 * ROW_HALO
EXT_COLS = COLS + 2 * COL_HALO
COARSE_COLS = EXT_COLS // RATIO
LANES = 384
SEGS = 16
LEN = EXT_COLS // SEGS
CLEN = LEN // 2
GROUPS = 8

sigma_now = 1.0
sigma_hat = 1.2
sigma_next = 0.4
sigma_data = 0.5
CHURN = math.sqrt(sigma_hat**2 - sigma_now**2)
DENOM = sigma_hat**2 + sigma_data**2
HALF = math.sqrt(0.5)
BF = jnp.bfloat16
F32 = jnp.float32


def silu(v):
    h = 0.5 * v
    return h + h * jnp.tanh(h)


def put_row(dst, row, val, n):
    dst[row, 1 : n + 1] = val.astype(BF)
    dst[row, 0] = pltpu.roll(val[n - 1], 1, 0).astype(BF)
    dst[row, n + 1] = pltpu.roll(val[0], SEGS - 1, 0).astype(BF)


def pair_rows(r, rows, top, bottom):
    mirrored = jnp.logical_or(
        jnp.logical_and(top == 1, r < 0), jnp.logical_and(bottom == 1, r >= rows)
    )
    return jnp.where(mirrored, r + 2, r - 1), jnp.where(mirrored, -1, 1)


def conv_pair(src, base, step, w, n):
    slabs = []
    for k in range(4):
        row = base + step * k
        for b in range(3):
            slabs.append(src[row, b : b + n].reshape(n * SEGS, CH))
    lhs = jnp.concatenate(slabs, axis=1)
    zero = jnp.zeros((3 * CH, CH), BF)
    rhs = jnp.concatenate(
        [jnp.concatenate([w[...], zero], 0), jnp.concatenate([zero, w[...]], 0)], 1
    )
    acc = jnp.dot(lhs, rhs, preferred_element_type=F32)
    return acc[:, :CH].reshape(n, SEGS, CH), acc[:, CH:].reshape(n, SEGS, CH)


def net_kernel(
    flags,
    x,
    cur,
    noise,
    w_in,
    w_f1,
    w_f2,
    w_c1,
    w_c2,
    w_out,
    out,
    a0,
    stem,
    act,
    hid,
    fine,
    pooled,
    cact,
    chid,
    merged,
    flat,
):
    top = flags[0]
    bottom = flags[1]

    i = lax.broadcasted_iota(jnp.int32, ((LEN + 2) * SEGS, LANES), 0)
    lane = lax.broadcasted_iota(jnp.int32, ((LEN + 2) * SEGS, LANES), 1)
    col = LEN * lax.rem(i, SEGS) + lax.div(i, SEGS) - 1
    inside = jnp.logical_and(col >= 0, col < EXT_COLS)
    hit = jnp.logical_or(lane == col, lane == EXT_COLS + lax.div(col, RATIO))
    place = jnp.where(jnp.logical_and(inside, hit), 1.0, 0.0).astype(BF)
    for g in range(GROUPS):
        part = x[96 * g : 96 * g + 128, :]
        val = lax.dot_general(place, part, (((1,), (1,)), ((), ())), preferred_element_type=F32)
        a0[g] = val.reshape(LEN + 2, SEGS, CH).astype(BF)

    act[0] = jnp.zeros((LEN + 2, SEGS, CH), BF)
    act[EXT_ROWS - 1] = jnp.zeros((LEN + 2, SEGS, CH), BF)
    chid[0] = jnp.zeros((CLEN + 2, SEGS, CH), BF)
    chid[21] = jnp.zeros((CLEN + 2, SEGS, CH), BF)

    def stem_body(g, carry):
        lhs = jnp.concatenate(
            [a0[g, b : b + LEN].reshape(LEN * SEGS, CH) for b in range(3)], axis=1
        )
        for j in range(3):
            r = 6 * g + 2 * j - 8
            _, step = pair_rows(r, ROWS, top, bottom)
            flip = jnp.where(step < 0, 1, 0)
            acc = jnp.dot(lhs, w_in[flip * 3 + j], preferred_element_type=F32)
            for h in range(2):
                val = acc[:, h * CH : (h + 1) * CH].reshape(LEN, SEGS, CH).astype(BF)
                stem[r + 8 + h] = val
                put_row(act, r + 9 + h, silu(val.astype(F32)), LEN)
        return carry

    lax.fori_loop(0, GROUPS, stem_body, 0)

    def first_body(p, carry):
        r = 2 * p - 8
        base, step = pair_rows(r, ROWS, top, bottom)
        o0, o1 = conv_pair(act, base + 9, step, w_f1, LEN)
        put_row(hid, base + step + 8, silu(o0), LEN)
        put_row(hid, base + 2 * step + 8, silu(o1), LEN)
        return carry

    lax.fori_loop(0, 24, first_body, 0)

    def second_body(p, carry):
        r = 2 * p - 6
        base, step = pair_rows(r, ROWS, top, bottom)
        o0, o1 = conv_pair(hid, base + 8, step, w_f2, LEN)
        r0 = base + step
        r1 = base + 2 * step
        v0 = ((stem[r0 + 8].astype(F32) + o0) * HALF).astype(BF)
        v1 = ((stem[r1 + 8].astype(F32) + o1) * HALF).astype(BF)
        fine[r0 + 6] = v0
        fine[r1 + 6] = v1
        both = (v0.astype(F32) + v1.astype(F32)).reshape(CLEN, 2, SEGS, CH)
        mean = ((both[:, 0] + both[:, 1]) * 0.25).astype(BF)
        pooled[p] = mean
        put_row(cact, p, silu(mean.astype(F32)), CLEN)
        return carry

    lax.fori_loop(0, 22, second_body, 0)

    def third_body(p, carry):
        r = 2 * p - 2
        base, step = pair_rows(r, ROWS // 2, top, bottom)
        o0, o1 = conv_pair(cact, base + 3, step, w_c1, CLEN)
        put_row(chid, base + step + 3, silu(o0), CLEN)
        put_row(chid, base + 2 * step + 3, silu(o1), CLEN)
        return carry

    lax.fori_loop(0, 10, third_body, 0)

    def fourth_body(p, carry):
        r = 2 * p - 2
        base, step = pair_rows(r, ROWS // 2, top, bottom)
        outs = conv_pair(chid, base + 3, step, w_c2, CLEN)
        for h in range(2):
            cr = base + (h + 1) * step
            co = ((pooled[cr + 3].astype(F32) + outs[h]) * HALF).astype(BF).astype(F32)
            wide = jnp.broadcast_to(co[:, None], (CLEN, 2, SEGS, CH)).reshape(LEN, SEGS, CH)
            for q in range(2):
                val = silu((fine[2 * cr + q + 6].astype(F32) + wide) * HALF)
                put_row(merged, 2 * cr + q + 4, val, LEN)
        return carry

    lax.fori_loop(0, 10, fourth_body, 0)

    group_lane = lax.broadcasted_iota(jnp.int32, (LEN, SEGS, CH), 2) // 32
    rhs = jnp.concatenate([w_out[:, k * CH : (k + 1) * CH] for k in range(10)], axis=0)
    total = jnp.zeros((LEN, SEGS, CH), F32)
    for g in range(4):
        lhs = jnp.concatenate(
            [
                merged[8 * g + 3 + k].reshape((LEN + 2) * SEGS, CH)
                for k in range(10)
            ],
            axis=1,
        )
        z = jnp.dot(lhs, rhs, preferred_element_type=F32).reshape(LEN + 2, SEGS, CH)
        shift = 32 * g
        val = pltpu.roll(z[:LEN], shift, 2) if shift else z[:LEN]
        val = val + pltpu.roll(z[1 : LEN + 1], (96 + shift) % CH, 2)
        val = val + pltpu.roll(z[2:], (64 + shift) % CH, 2)
        total = jnp.where(group_lane == g, val, total)
    for l in range(LEN):
        flat[pl.ds(l, SEGS, stride=LEN), :] = total[l]
    rows = flat[COL_HALO : COL_HALO + COLS, :].T
    for g in range(4):
        for o in range(4):
            network = rows[32 * g + 8 * o : 32 * g + 8 * o + 8]
            at = pl.ds(8 * g, 8)
            perturbed = cur[o, at] + CHURN * noise[o, at]
            denoised = (
                sigma_data**2 / DENOM * perturbed
                + sigma_hat * sigma_data / math.sqrt(DENOM) * network
            )
            out[o, at] = perturbed + (sigma_next - sigma_hat) / sigma_hat * (perturbed - denoised)


def run_net(flags, x, cur, noise, w_in, w_f1, w_f2, w_c1, w_c2, w_out):
    vmem = pl.BlockSpec(memory_space=pltpu.VMEM)
    row = (LEN + 2, SEGS, CH)
    crow = (CLEN + 2, SEGS, CH)
    return pl.pallas_call(
        net_kernel,
        out_shape=jax.ShapeDtypeStruct((4, ROWS, COLS), F32),
        in_specs=[pl.BlockSpec(memory_space=pltpu.SMEM)] + [vmem] * 9,
        out_specs=vmem,
        scratch_shapes=[
            pltpu.VMEM((GROUPS,) + row, BF),
            pltpu.VMEM((48, LEN, SEGS, CH), BF),
            pltpu.VMEM((EXT_ROWS,) + row, BF),
            pltpu.VMEM((48,) + row, BF),
            pltpu.VMEM((44, LEN, SEGS, CH), BF),
            pltpu.VMEM((22, CLEN, SEGS, CH), BF),
            pltpu.VMEM((22,) + crow, BF),
            pltpu.VMEM((22,) + crow, BF),
            pltpu.VMEM((40,) + row, BF),
            pltpu.VMEM((EXT_COLS, CH), F32),
        ],
        compiler_params=pltpu.CompilerParams(vmem_limit_bytes=60000 * 1024),
        name="net",
    )(flags, x, cur, noise, w_in, w_f1, w_f2, w_c1, w_c2, w_out)


def stem_weights(kernel):
    tables = []
    for k in (kernel, kernel[::-1]):
        k = k.transpose(1, 0, 2, 3)
        for j in range(3):
            first = jnp.pad(k, ((0, 0), (2 * j, 5 - 2 * j), (0, 0), (0, 0)))
            second = jnp.pad(k, ((0, 0), (2 * j + 1, 4 - 2 * j), (0, 0), (0, 0)))
            tables.append(jnp.concatenate([first, second], axis=3).reshape(3 * 8 * 16, 2 * CH))
    return jnp.stack(tables)


def output_weights(kernel):
    per_row = []
    for r in range(8):
        per_row.append(jnp.pad(kernel, ((r, 7 - r), (0, 0), (0, 0), (0, 0))))
    w = jnp.stack(per_row)
    w = w.transpose(3, 1, 2, 4, 0).reshape(CH, 10, 96)
    return jnp.pad(w, ((0, 0), (0, 0), (0, 32))).reshape(CH, 10 * CH)


def swap(block, pairs):
    return lax.ppermute(block, ("lat", "lon"), pairs)


def device(lat, lon):
    return lat * 16 + lon % 16


def exchange(net_in, coarse, tile_owner, lat):
    first = net_in[:, :ROW_HALO]
    last = net_in[:, ROWS - ROW_HALO :]
    dest = lax.broadcasted_iota(jnp.int32, (16, 1, 1, 1), 0)
    rows = jnp.where(
        dest == lat + 1, last[None], jnp.where(dest == lat - 1, first[None], jnp.zeros_like(first[None]))
    )
    sent = jnp.concatenate(
        [rows.reshape(16, 72, CH), jnp.broadcast_to(coarse.reshape(1, 12, CH), (16, 12, CH))], axis=1
    )
    got = lax.all_to_all(sent, "lat", 0, 0, tiled=True)
    above = jnp.maximum(lat - 1, 0)
    below = jnp.minimum(lat + 1, 15)

    def rows_from(i):
        return lax.dynamic_slice_in_dim(got, i, 1, 0)[0, :72].reshape(4, ROW_HALO, COLS)

    def coarse_from(i):
        slot = tile_owner[i]
        return lax.dynamic_slice_in_dim(got, slot, 1, 0)[0, 72:].reshape(12, 4, 32)

    own = coarse_from(lat)
    north, south = rows_from(above), rows_from(below)
    cnorth, csouth = coarse_from(above)[:, 2:], coarse_from(below)[:, :2]

    is_top, is_bottom = lat == 0, lat == 15
    pole = jnp.where(is_top, first, last)
    cpole = jnp.where(is_top, own[:, :2], own[:, 2:])
    packed = jnp.concatenate([pole.reshape(72, CH), cpole.reshape(6, CH)], axis=0)
    across = swap(
        packed, [(device(i, q), device(i, q + 8)) for i in (0, 15) for q in range(16)]
    )
    pole = across[:72].reshape(4, ROW_HALO, COLS)[:, ::-1]
    cpole = across[72:].reshape(12, 2, 32)[:, ::-1]
    north = jnp.where(is_top, pole, north)
    south = jnp.where(is_bottom, pole, south)
    cnorth = jnp.where(is_top, cpole, cnorth)
    csouth = jnp.where(is_bottom, cpole, csouth)
    tall = jnp.concatenate([north, net_in, south], axis=1)
    ctall = jnp.concatenate([cnorth, own, csouth], axis=1)

    def pack(fine, crs):
        flat = jnp.concatenate([fine.reshape(-1), crs.reshape(-1)])
        return jnp.pad(flat, (0, 27 * CH - flat.shape[0])).reshape(27, CH)

    def unpack(block):
        flat = block.reshape(-1)
        n = 4 * EXT_ROWS * COL_HALO
        return flat[:n].reshape(4, EXT_ROWS, COL_HALO), flat[n : n + 12 * 8 * 2].reshape(12, 8, 2)

    east = pack(tall[:, :, COLS - COL_HALO :], ctall[:, :, 30:])
    west = pack(tall[:, :, :COL_HALO], ctall[:, :, :2])
    odd = lax.axis_index("lon") % 2 == 1
    near = swap(
        jnp.where(odd, west, east), [(device(i, q), device(i, q ^ 1)) for i in range(16) for q in range(16)]
    )
    far = swap(
        jnp.where(odd, east, west),
        [(device(i, q), device(i, q + 1 if q % 2 else q - 1)) for i in range(16) for q in range(16)],
    )
    left, cleft = unpack(jnp.where(odd, near, far))
    right, cright = unpack(jnp.where(odd, far, near))
    wide = jnp.concatenate([left, tall, right], axis=2)
    cwide = jnp.concatenate([cleft, ctall, cright], axis=2)
    wide = jnp.pad(wide, ((0, 0), (0, 0), (0, LANES - EXT_COLS))).transpose(1, 0, 2)
    cwide = jnp.pad(cwide, ((0, 0), (0, 0), (EXT_COLS, LANES - EXT_COLS - COARSE_COLS))).transpose(1, 0, 2)
    cwide = jnp.repeat(cwide, RATIO, axis=0)[RATIO - 1 : RATIO - 1 + EXT_ROWS]
    return jnp.concatenate([wide, cwide], axis=1).reshape(EXT_ROWS * 16, LANES)


def body(
    current_sample,
    churn_noise,
    coarse_fields,
    tile_owner,
    input_kernel,
    fine_first,
    fine_second,
    coarse_first,
    coarse_second,
    output_kernel,
):
    lat = lax.axis_index("lat")
    scale_in = 1.0 / math.sqrt(DENOM)
    net_in = ((current_sample + CHURN * churn_noise) * scale_in).astype(BF)
    x = exchange(net_in, coarse_fields.astype(BF), tile_owner, lat)
    flags = jnp.stack([(lat == 0).astype(jnp.int32), (lat == 15).astype(jnp.int32)])
    return run_net(
        flags,
        x,
        current_sample,
        churn_noise,
        stem_weights(input_kernel),
        fine_first.reshape(9 * CH, CH),
        fine_second.reshape(9 * CH, CH),
        coarse_first.reshape(9 * CH, CH),
        coarse_second.reshape(9 * CH, CH),
        output_weights(output_kernel),
    )


def solution(mesh):
    placed = (P(None, "lat", "lon"),) * 3 + (P(),) * 7
    return jax.shard_map(
        body, mesh=mesh, in_specs=placed, out_specs=P(None, "lat", "lon"), check_vma=False
    )
```

```python
import math

import jax
import jax.numpy as jnp
from jax import lax
from jax.experimental import pallas as pl
from jax.experimental.pallas import tpu as pltpu
from jax.sharding import PartitionSpec as P

RATIO = 8
CH = 128
ROWS = 32
COLS = 256
ROW_HALO = 9
COL_HALO = 16
EXT_ROWS = ROWS + 2 * ROW_HALO
EXT_COLS = COLS + 2 * COL_HALO
COARSE_COLS = EXT_COLS // RATIO
LANES = 384
SEGS = 16
LEN = EXT_COLS // SEGS
CLEN = LEN // 2
GROUPS = 8
NF, NF2, NC = 4, 4, 5
N1, N2, N3 = 24 // NF, 22 // NF2, 10 // NC

sigma_now = 1.0
sigma_hat = 1.2
sigma_next = 0.4
sigma_data = 0.5
CHURN = math.sqrt(sigma_hat**2 - sigma_now**2)
DENOM = sigma_hat**2 + sigma_data**2
HALF = math.sqrt(0.5)
BF = jnp.bfloat16
F32 = jnp.float32


def silu(v):
    h = 0.5 * v
    return h + h * jnp.tanh(h)


def put_row(dst, row, val, n):
    dst[row, 1 : n + 1] = val.astype(BF)
    dst[row, 0] = pltpu.roll(val[n - 1], 1, 0).astype(BF)
    dst[row, n + 1] = pltpu.roll(val[0], SEGS - 1, 0).astype(BF)


def pair_rows(r, rows, top, bottom):
    mirrored = jnp.logical_or(
        jnp.logical_and(top == 1, r < 0), jnp.logical_and(bottom == 1, r >= rows)
    )
    return jnp.where(mirrored, r + 2, r - 1), jnp.where(mirrored, -1, 1)


def conv_pairs(src, firsts, w, n):
    lhs = jnp.concatenate(
        [
            jnp.concatenate(
                [
                    src[base + step * k, b : b + n].reshape(n * SEGS, CH)
                    for k in range(4)
                    for b in range(3)
                ],
                axis=1,
            )
            for base, step in firsts
        ],
        axis=0,
    )
    zero = jnp.zeros((3 * CH, CH), BF)
    rhs = jnp.concatenate(
        [jnp.concatenate([w[...], zero], 0), jnp.concatenate([zero, w[...]], 0)], 1
    )
    acc = jnp.dot(lhs, rhs, preferred_element_type=F32).reshape(len(firsts), n, SEGS, 2 * CH)
    return [(acc[i, :, :, :CH], acc[i, :, :, CH:]) for i in range(len(firsts))]


def net_kernel(
    flags,
    x,
    cur,
    noise,
    w_in,
    w_f1,
    w_f2,
    w_c1,
    w_c2,
    w_out,
    out,
    a0,
    stem,
    act,
    hid,
    fine,
    pooled,
    cact,
    chid,
    merged,
    flat,
):
    top = flags[0]
    bottom = flags[1]

    i = lax.broadcasted_iota(jnp.int32, ((LEN + 2) * SEGS, LANES), 0)
    lane = lax.broadcasted_iota(jnp.int32, ((LEN + 2) * SEGS, LANES), 1)
    col = LEN * lax.rem(i, SEGS) + lax.div(i, SEGS) - 1
    inside = jnp.logical_and(col >= 0, col < EXT_COLS)
    hit = jnp.logical_or(lane == col, lane == EXT_COLS + lax.div(col, RATIO))
    place = jnp.where(jnp.logical_and(inside, hit), 1.0, 0.0).astype(BF)
    for g in range(GROUPS):
        part = x[96 * g : 96 * g + 128, :]
        val = lax.dot_general(place, part, (((1,), (1,)), ((), ())), preferred_element_type=F32)
        a0[g] = val.reshape(LEN + 2, SEGS, CH).astype(BF)

    act[0] = jnp.zeros((LEN + 2, SEGS, CH), BF)
    act[EXT_ROWS - 1] = jnp.zeros((LEN + 2, SEGS, CH), BF)
    chid[0] = jnp.zeros((CLEN + 2, SEGS, CH), BF)
    chid[21] = jnp.zeros((CLEN + 2, SEGS, CH), BF)

    def stem_body(g, carry):
        lhs = jnp.concatenate(
            [a0[g, b : b + LEN].reshape(LEN * SEGS, CH) for b in range(3)], axis=1
        )
        for j in range(3):
            r = 6 * g + 2 * j - 8
            _, step = pair_rows(r, ROWS, top, bottom)
            flip = jnp.where(step < 0, 1, 0)
            acc = jnp.dot(lhs, w_in[flip * 3 + j], preferred_element_type=F32)
            for h in range(2):
                val = acc[:, h * CH : (h + 1) * CH].reshape(LEN, SEGS, CH).astype(BF)
                stem[r + 8 + h] = val
                put_row(act, r + 9 + h, silu(val.astype(F32)), LEN)
        return carry

    lax.fori_loop(0, GROUPS, stem_body, 0)

    def first_body(p, carry):
        firsts = [pair_rows(2 * NF * p + 2 * i - 8, ROWS, top, bottom) for i in range(NF)]
        outs = conv_pairs(act, [(base + 9, step) for base, step in firsts], w_f1, LEN)
        for (base, step), (o0, o1) in zip(firsts, outs):
            put_row(hid, base + step + 8, silu(o0), LEN)
            put_row(hid, base + 2 * step + 8, silu(o1), LEN)
        return carry

    lax.fori_loop(0, N1, first_body, 0)

    def second_pairs(first, count):
        firsts = [pair_rows(2 * (first + i) - 6, ROWS, top, bottom) for i in range(count)]
        outs = conv_pairs(hid, [(base + 8, step) for base, step in firsts], w_f2, LEN)
        for i, ((base, step), (o0, o1)) in enumerate(zip(firsts, outs)):
            r0 = base + step
            r1 = base + 2 * step
            v0 = ((stem[r0 + 8].astype(F32) + o0) * HALF).astype(BF)
            v1 = ((stem[r1 + 8].astype(F32) + o1) * HALF).astype(BF)
            fine[r0 + 6] = v0
            fine[r1 + 6] = v1
            both = (v0.astype(F32) + v1.astype(F32)).reshape(CLEN, 2, SEGS, CH)
            mean = ((both[:, 0] + both[:, 1]) * 0.25).astype(BF)
            pooled[first + i] = mean
            put_row(cact, first + i, silu(mean.astype(F32)), CLEN)

    def second_body(p, carry):
        second_pairs(NF2 * p, NF2)
        return carry

    lax.fori_loop(0, N2, second_body, 0)
    second_pairs(NF2 * N2, 22 - NF2 * N2)

    def third_body(p, carry):
        firsts = [pair_rows(2 * NC * p + 2 * i - 2, ROWS // 2, top, bottom) for i in range(NC)]
        outs = conv_pairs(cact, [(base + 3, step) for base, step in firsts], w_c1, CLEN)
        for (base, step), (o0, o1) in zip(firsts, outs):
            put_row(chid, base + step + 3, silu(o0), CLEN)
            put_row(chid, base + 2 * step + 3, silu(o1), CLEN)
        return carry

    lax.fori_loop(0, N3, third_body, 0)

    def fourth_body(p, carry):
        firsts = [pair_rows(2 * NC * p + 2 * i - 2, ROWS // 2, top, bottom) for i in range(NC)]
        results = conv_pairs(chid, [(base + 3, step) for base, step in firsts], w_c2, CLEN)
        for (base, step), outs in zip(firsts, results):
            for h in range(2):
                cr = base + (h + 1) * step
                co = ((pooled[cr + 3].astype(F32) + outs[h]) * HALF).astype(BF).astype(F32)
                wide = jnp.broadcast_to(co[:, None], (CLEN, 2, SEGS, CH)).reshape(LEN, SEGS, CH)
                for q in range(2):
                    val = silu((fine[2 * cr + q + 6].astype(F32) + wide) * HALF)
                    put_row(merged, 2 * cr + q + 4, val, LEN)
        return carry

    lax.fori_loop(0, N3, fourth_body, 0)

    group_lane = lax.broadcasted_iota(jnp.int32, (LEN, SEGS, CH), 2) // 32
    rhs = jnp.concatenate([w_out[:, k * CH : (k + 1) * CH] for k in range(10)], axis=0)
    total = jnp.zeros((LEN, SEGS, CH), F32)
    for g in range(4):
        lhs = jnp.concatenate(
            [
                merged[8 * g + 3 + k].reshape((LEN + 2) * SEGS, CH)
                for k in range(10)
            ],
            axis=1,
        )
        z = jnp.dot(lhs, rhs, preferred_element_type=F32).reshape(LEN + 2, SEGS, CH)
        shift = 32 * g
        val = pltpu.roll(z[:LEN], shift, 2) if shift else z[:LEN]
        val = val + pltpu.roll(z[1 : LEN + 1], (96 + shift) % CH, 2)
        val = val + pltpu.roll(z[2:], (64 + shift) % CH, 2)
        total = jnp.where(group_lane == g, val, total)
    for l in range(LEN):
        flat[pl.ds(l, SEGS, stride=LEN), :] = total[l]
    rows = flat[COL_HALO : COL_HALO + COLS, :].T
    for g in range(4):
        for o in range(4):
            network = rows[32 * g + 8 * o : 32 * g + 8 * o + 8]
            at = pl.ds(8 * g, 8)
            perturbed = cur[o, at] + CHURN * noise[o, at]
            denoised = (
                sigma_data**2 / DENOM * perturbed
                + sigma_hat * sigma_data / math.sqrt(DENOM) * network
            )
            out[o, at] = perturbed + (sigma_next - sigma_hat) / sigma_hat * (perturbed - denoised)


def run_net(flags, x, cur, noise, w_in, w_f1, w_f2, w_c1, w_c2, w_out):
    vmem = pl.BlockSpec(memory_space=pltpu.VMEM)
    row = (LEN + 2, SEGS, CH)
    crow = (CLEN + 2, SEGS, CH)
    return pl.pallas_call(
        net_kernel,
        out_shape=jax.ShapeDtypeStruct((4, ROWS, COLS), F32),
        in_specs=[pl.BlockSpec(memory_space=pltpu.SMEM)] + [vmem] * 9,
        out_specs=vmem,
        scratch_shapes=[
            pltpu.VMEM((GROUPS,) + row, BF),
            pltpu.VMEM((48, LEN, SEGS, CH), BF),
            pltpu.VMEM((EXT_ROWS,) + row, BF),
            pltpu.VMEM((48,) + row, BF),
            pltpu.VMEM((44, LEN, SEGS, CH), BF),
            pltpu.VMEM((22, CLEN, SEGS, CH), BF),
            pltpu.VMEM((22,) + crow, BF),
            pltpu.VMEM((22,) + crow, BF),
            pltpu.VMEM((40,) + row, BF),
            pltpu.VMEM((EXT_COLS, CH), F32),
        ],
        compiler_params=pltpu.CompilerParams(vmem_limit_bytes=60000 * 1024),
        name="net",
    )(flags, x, cur, noise, w_in, w_f1, w_f2, w_c1, w_c2, w_out)


def stem_weights(kernel):
    tables = []
    for k in (kernel, kernel[::-1]):
        k = k.transpose(1, 0, 2, 3)
        for j in range(3):
            first = jnp.pad(k, ((0, 0), (2 * j, 5 - 2 * j), (0, 0), (0, 0)))
            second = jnp.pad(k, ((0, 0), (2 * j + 1, 4 - 2 * j), (0, 0), (0, 0)))
            tables.append(jnp.concatenate([first, second], axis=3).reshape(3 * 8 * 16, 2 * CH))
    return jnp.stack(tables)


def output_weights(kernel):
    per_row = []
    for r in range(8):
        per_row.append(jnp.pad(kernel, ((r, 7 - r), (0, 0), (0, 0), (0, 0))))
    w = jnp.stack(per_row)
    w = w.transpose(3, 1, 2, 4, 0).reshape(CH, 10, 96)
    return jnp.pad(w, ((0, 0), (0, 0), (0, 32))).reshape(CH, 10 * CH)


def swap(block, pairs):
    return lax.ppermute(block, ("lat", "lon"), pairs)


def device(lat, lon):
    return lat * 16 + lon % 16


def exchange(net_in, coarse, tile_owner, lat):
    first = net_in[:, :ROW_HALO]
    last = net_in[:, ROWS - ROW_HALO :]
    dest = lax.broadcasted_iota(jnp.int32, (16, 1, 1, 1), 0)
    rows = jnp.where(
        dest == lat + 1, last[None], jnp.where(dest == lat - 1, first[None], jnp.zeros_like(first[None]))
    )
    sent = jnp.concatenate(
        [rows.reshape(16, 72, CH), jnp.broadcast_to(coarse.reshape(1, 12, CH), (16, 12, CH))], axis=1
    )
    got = lax.all_to_all(sent, "lat", 0, 0, tiled=True)
    above = jnp.maximum(lat - 1, 0)
    below = jnp.minimum(lat + 1, 15)

    def rows_from(i):
        return lax.dynamic_slice_in_dim(got, i, 1, 0)[0, :72].reshape(4, ROW_HALO, COLS)

    def coarse_from(i):
        slot = tile_owner[i]
        return lax.dynamic_slice_in_dim(got, slot, 1, 0)[0, 72:].reshape(12, 4, 32)

    own = coarse_from(lat)
    north, south = rows_from(above), rows_from(below)
    cnorth, csouth = coarse_from(above)[:, 2:], coarse_from(below)[:, :2]

    is_top, is_bottom = lat == 0, lat == 15
    pole = jnp.where(is_top, first, last)
    cpole = jnp.where(is_top, own[:, :2], own[:, 2:])
    packed = jnp.concatenate([pole.reshape(72, CH), cpole.reshape(6, CH)], axis=0)
    across = swap(
        packed, [(device(i, q), device(i, q + 8)) for i in (0, 15) for q in range(16)]
    )
    pole = across[:72].reshape(4, ROW_HALO, COLS)[:, ::-1]
    cpole = across[72:].reshape(12, 2, 32)[:, ::-1]
    north = jnp.where(is_top, pole, north)
    south = jnp.where(is_bottom, pole, south)
    cnorth = jnp.where(is_top, cpole, cnorth)
    csouth = jnp.where(is_bottom, cpole, csouth)
    tall = jnp.concatenate([north, net_in, south], axis=1)
    ctall = jnp.concatenate([cnorth, own, csouth], axis=1)

    def pack(fine, crs):
        flat = jnp.concatenate([fine.reshape(-1), crs.reshape(-1)])
        return jnp.pad(flat, (0, 27 * CH - flat.shape[0])).reshape(27, CH)

    def unpack(block):
        flat = block.reshape(-1)
        n = 4 * EXT_ROWS * COL_HALO
        return flat[:n].reshape(4, EXT_ROWS, COL_HALO), flat[n : n + 12 * 8 * 2].reshape(12, 8, 2)

    east = pack(tall[:, :, COLS - COL_HALO :], ctall[:, :, 30:])
    west = pack(tall[:, :, :COL_HALO], ctall[:, :, :2])
    odd = lax.axis_index("lon") % 2 == 1
    near = swap(
        jnp.where(odd, west, east), [(device(i, q), device(i, q ^ 1)) for i in range(16) for q in range(16)]
    )
    far = swap(
        jnp.where(odd, east, west),
        [(device(i, q), device(i, q + 1 if q % 2 else q - 1)) for i in range(16) for q in range(16)],
    )
    left, cleft = unpack(jnp.where(odd, near, far))
    right, cright = unpack(jnp.where(odd, far, near))
    wide = jnp.concatenate([left, tall, right], axis=2)
    cwide = jnp.concatenate([cleft, ctall, cright], axis=2)
    wide = jnp.pad(wide, ((0, 0), (0, 0), (0, LANES - EXT_COLS))).transpose(1, 0, 2)
    cwide = jnp.pad(cwide, ((0, 0), (0, 0), (EXT_COLS, LANES - EXT_COLS - COARSE_COLS))).transpose(1, 0, 2)
    cwide = jnp.repeat(cwide, RATIO, axis=0)[RATIO - 1 : RATIO - 1 + EXT_ROWS]
    return jnp.concatenate([wide, cwide], axis=1).reshape(EXT_ROWS * 16, LANES)


def body(
    current_sample,
    churn_noise,
    coarse_fields,
    tile_owner,
    input_kernel,
    fine_first,
    fine_second,
    coarse_first,
    coarse_second,
    output_kernel,
):
    lat = lax.axis_index("lat")
    scale_in = 1.0 / math.sqrt(DENOM)
    net_in = ((current_sample + CHURN * churn_noise) * scale_in).astype(BF)
    x = exchange(net_in, coarse_fields.astype(BF), tile_owner, lat)
    flags = jnp.stack([(lat == 0).astype(jnp.int32), (lat == 15).astype(jnp.int32)])
    return run_net(
        flags,
        x,
        current_sample,
        churn_noise,
        stem_weights(input_kernel),
        fine_first.reshape(9 * CH, CH),
        fine_second.reshape(9 * CH, CH),
        coarse_first.reshape(9 * CH, CH),
        coarse_second.reshape(9 * CH, CH),
        output_weights(output_kernel),
    )


def solution(mesh):
    placed = (P(None, "lat", "lon"),) * 3 + (P(),) * 7
    return jax.shard_map(
        body, mesh=mesh, in_specs=placed, out_specs=P(None, "lat", "lon"), check_vma=False
    )
```

```python
import math

import jax
import jax.numpy as jnp
from jax import lax
from jax.experimental import pallas as pl
from jax.experimental.pallas import tpu as pltpu
from jax.sharding import PartitionSpec as P


RATIO = 8
CH = 128
ROWS = 32
COLS = 256
ROW_HALO = 9
COL_HALO = 16
EXT_ROWS = ROWS + 2 * ROW_HALO
EXT_COLS = COLS + 2 * COL_HALO
COARSE_COLS = EXT_COLS // RATIO
LANES = 384
SEGS = 16
LEN = EXT_COLS // SEGS
CLEN = LEN // 2
GROUPS = 8
NF, NF2, NC = 4, 4, 5
N1, N2, N3 = 24 // NF, 22 // NF2, 10 // NC

sigma_now = 1.0
sigma_hat = 1.2
sigma_next = 0.4
sigma_data = 0.5
CHURN = math.sqrt(sigma_hat**2 - sigma_now**2)
DENOM = sigma_hat**2 + sigma_data**2
HALF = math.sqrt(0.5)
BF = jnp.bfloat16
F32 = jnp.float32


def silu(v):
    h = 0.5 * v
    return h + h * jnp.tanh(h)


def put_row(dst, row, val, n):
    dst[row, 1 : n + 1] = val.astype(BF)
    dst[row, 0] = pltpu.roll(val[n - 1], 1, 0).astype(BF)
    dst[row, n + 1] = pltpu.roll(val[0], SEGS - 1, 0).astype(BF)


def pair_rows(r, rows, top, bottom):
    mirrored = jnp.logical_or(
        jnp.logical_and(top == 1, r < 0), jnp.logical_and(bottom == 1, r >= rows)
    )
    return jnp.where(mirrored, r + 2, r - 1), jnp.where(mirrored, -1, 1)


def conv_pairs(src, firsts, w, n):
    lhs = jnp.concatenate(
        [
            jnp.concatenate(
                [
                    src[base + step * k, b : b + n].reshape(n * SEGS, CH)
                    for k in range(4)
                    for b in range(3)
                ],
                axis=1,
            )
            for base, step in firsts
        ],
        axis=0,
    )
    zero = jnp.zeros((3 * CH, CH), BF)
    rhs = jnp.concatenate(
        [jnp.concatenate([w[...], zero], 0), jnp.concatenate([zero, w[...]], 0)], 1
    )
    acc = jnp.dot(lhs, rhs, preferred_element_type=F32).reshape(len(firsts), n, SEGS, 2 * CH)
    return [(acc[i, :, :, :CH], acc[i, :, :, CH:]) for i in range(len(firsts))]


def net_kernel(
    flags,
    x,
    cur,
    noise,
    w_in,
    w_f1,
    w_f2,
    w_c1,
    w_c2,
    w_out,
    out,
    a0,
    stem,
    act,
    hid,
    fine,
    pooled,
    cact,
    chid,
    merged,
    flat,
):
    top = flags[0]
    bottom = flags[1]

    i = lax.broadcasted_iota(jnp.int32, ((LEN + 2) * SEGS, LANES), 0)
    lane = lax.broadcasted_iota(jnp.int32, ((LEN + 2) * SEGS, LANES), 1)
    col = LEN * (i & (SEGS - 1)) + (i >> 4) - 1
    inside = jnp.logical_and(col >= 0, col < EXT_COLS)
    hit = jnp.logical_or(lane == col, lane == EXT_COLS + (col >> 3))
    place = jnp.where(jnp.logical_and(inside, hit), 1.0, 0.0).astype(BF)
    for g in range(GROUPS):
        part = x[96 * g : 96 * g + 128, :]
        val = lax.dot_general(place, part, (((1,), (1,)), ((), ())), preferred_element_type=F32)
        a0[g] = val.reshape(LEN + 2, SEGS, CH).astype(BF)

    act[0] = jnp.zeros((LEN + 2, SEGS, CH), BF)
    act[EXT_ROWS - 1] = jnp.zeros((LEN + 2, SEGS, CH), BF)
    chid[0] = jnp.zeros((CLEN + 2, SEGS, CH), BF)
    chid[21] = jnp.zeros((CLEN + 2, SEGS, CH), BF)

    def stem_body(g, carry):
        lhs = jnp.concatenate(
            [a0[g, b : b + LEN].reshape(LEN * SEGS, CH) for b in range(3)], axis=1
        )
        for j in range(3):
            r = 6 * g + 2 * j - 8
            _, step = pair_rows(r, ROWS, top, bottom)
            flip = jnp.where(step < 0, 1, 0)
            acc = jnp.dot(lhs, w_in[flip * 3 + j], preferred_element_type=F32)
            for h in range(2):
                val = acc[:, h * CH : (h + 1) * CH].reshape(LEN, SEGS, CH).astype(BF)
                stem[r + 8 + h] = val
                put_row(act, r + 9 + h, silu(val.astype(F32)), LEN)
        return carry

    lax.fori_loop(0, GROUPS, stem_body, 0)

    def first_body(p, carry):
        firsts = [pair_rows(2 * NF * p + 2 * i - 8, ROWS, top, bottom) for i in range(NF)]
        outs = conv_pairs(act, [(base + 9, step) for base, step in firsts], w_f1, LEN)
        for (base, step), (o0, o1) in zip(firsts, outs):
            put_row(hid, base + step + 8, silu(o0), LEN)
            put_row(hid, base + 2 * step + 8, silu(o1), LEN)
        return carry

    lax.fori_loop(0, N1, first_body, 0)

    def second_pairs(first, count):
        firsts = [pair_rows(2 * (first + i) - 6, ROWS, top, bottom) for i in range(count)]
        outs = conv_pairs(hid, [(base + 8, step) for base, step in firsts], w_f2, LEN)
        for i, ((base, step), (o0, o1)) in enumerate(zip(firsts, outs)):
            r0 = base + step
            r1 = base + 2 * step
            v0 = ((stem[r0 + 8].astype(F32) + o0) * HALF).astype(BF)
            v1 = ((stem[r1 + 8].astype(F32) + o1) * HALF).astype(BF)
            fine[r0 + 6] = v0
            fine[r1 + 6] = v1
            both = (v0.astype(F32) + v1.astype(F32)).reshape(CLEN, 2, SEGS, CH)
            mean = ((both[:, 0] + both[:, 1]) * 0.25).astype(BF)
            pooled[first + i] = mean
            put_row(cact, first + i, silu(mean.astype(F32)), CLEN)

    def second_body(p, carry):
        second_pairs(NF2 * p, NF2)
        return carry

    lax.fori_loop(0, N2, second_body, 0)
    second_pairs(NF2 * N2, 22 - NF2 * N2)

    def third_body(p, carry):
        firsts = [pair_rows(2 * NC * p + 2 * i - 2, ROWS // 2, top, bottom) for i in range(NC)]
        outs = conv_pairs(cact, [(base + 3, step) for base, step in firsts], w_c1, CLEN)
        for (base, step), (o0, o1) in zip(firsts, outs):
            put_row(chid, base + step + 3, silu(o0), CLEN)
            put_row(chid, base + 2 * step + 3, silu(o1), CLEN)
        return carry

    lax.fori_loop(0, N3, third_body, 0)

    def fourth_body(p, carry):
        firsts = [pair_rows(2 * NC * p + 2 * i - 2, ROWS // 2, top, bottom) for i in range(NC)]
        results = conv_pairs(chid, [(base + 3, step) for base, step in firsts], w_c2, CLEN)
        for (base, step), outs in zip(firsts, results):
            for h in range(2):
                cr = base + (h + 1) * step
                co = ((pooled[cr + 3].astype(F32) + outs[h]) * HALF).astype(BF).astype(F32)
                wide = jnp.broadcast_to(co[:, None], (CLEN, 2, SEGS, CH)).reshape(LEN, SEGS, CH)
                for q in range(2):
                    val = silu((fine[2 * cr + q + 6].astype(F32) + wide) * HALF)
                    put_row(merged, 2 * cr + q + 4, val, LEN)
        return carry

    lax.fori_loop(0, N3, fourth_body, 0)

    group_lane = lax.broadcasted_iota(jnp.int32, (LEN, SEGS, CH), 2) // 32
    rhs = jnp.concatenate([w_out[:, k * CH : (k + 1) * CH] for k in range(10)], axis=0)
    total = jnp.zeros((LEN, SEGS, CH), F32)
    for g in range(4):
        lhs = jnp.concatenate(
            [
                merged[8 * g + 3 + k].reshape((LEN + 2) * SEGS, CH)
                for k in range(10)
            ],
            axis=1,
        )
        z = jnp.dot(lhs, rhs, preferred_element_type=F32).reshape(LEN + 2, SEGS, CH)
        shift = 32 * g
        val = pltpu.roll(z[:LEN], shift, 2) if shift else z[:LEN]
        val = val + pltpu.roll(z[1 : LEN + 1], (96 + shift) % CH, 2)
        val = val + pltpu.roll(z[2:], (64 + shift) % CH, 2)
        total = jnp.where(group_lane == g, val, total)
    for l in range(LEN):
        flat[pl.ds(l, SEGS, stride=LEN), :] = total[l]
    rows = flat[COL_HALO : COL_HALO + COLS, :].T
    for g in range(4):
        for o in range(4):
            network = rows[32 * g + 8 * o : 32 * g + 8 * o + 8]
            at = pl.ds(8 * g, 8)
            perturbed = cur[o, at] + CHURN * noise[o, at]
            denoised = (
                sigma_data**2 / DENOM * perturbed
                + sigma_hat * sigma_data / math.sqrt(DENOM) * network
            )
            out[o, at] = perturbed + (sigma_next - sigma_hat) / sigma_hat * (perturbed - denoised)


def run_net(flags, x, cur, noise, w_in, w_f1, w_f2, w_c1, w_c2, w_out):
    vmem = pl.BlockSpec(memory_space=pltpu.VMEM)
    row = (LEN + 2, SEGS, CH)
    crow = (CLEN + 2, SEGS, CH)
    return pl.pallas_call(
        net_kernel,
        out_shape=jax.ShapeDtypeStruct((4, ROWS, COLS), F32),
        in_specs=[pl.BlockSpec(memory_space=pltpu.SMEM)] + [vmem] * 9,
        out_specs=vmem,
        scratch_shapes=[
            pltpu.VMEM((GROUPS,) + row, BF),
            pltpu.VMEM((48, LEN, SEGS, CH), BF),
            pltpu.VMEM((EXT_ROWS,) + row, BF),
            pltpu.VMEM((48,) + row, BF),
            pltpu.VMEM((44, LEN, SEGS, CH), BF),
            pltpu.VMEM((22, CLEN, SEGS, CH), BF),
            pltpu.VMEM((22,) + crow, BF),
            pltpu.VMEM((22,) + crow, BF),
            pltpu.VMEM((40,) + row, BF),
            pltpu.VMEM((EXT_COLS, CH), F32),
        ],
        compiler_params=pltpu.CompilerParams(vmem_limit_bytes=58 * 1024 * 1024),
        name="net",
    )(flags, x, cur, noise, w_in, w_f1, w_f2, w_c1, w_c2, w_out)


def stem_weights(kernel):
    tables = []
    for k in (kernel, kernel[::-1]):
        k = k.transpose(1, 0, 2, 3)
        for j in range(3):
            first = jnp.pad(k, ((0, 0), (2 * j, 5 - 2 * j), (0, 0), (0, 0)))
            second = jnp.pad(k, ((0, 0), (2 * j + 1, 4 - 2 * j), (0, 0), (0, 0)))
            tables.append(jnp.concatenate([first, second], axis=3).reshape(3 * 8 * 16, 2 * CH))
    return jnp.stack(tables)


def output_weights(kernel):
    per_row = []
    for r in range(8):
        per_row.append(jnp.pad(kernel, ((r, 7 - r), (0, 0), (0, 0), (0, 0))))
    w = jnp.stack(per_row)
    w = w.transpose(3, 1, 2, 4, 0).reshape(CH, 10, 96)
    return jnp.pad(w, ((0, 0), (0, 0), (0, 32))).reshape(CH, 10 * CH)


def swap(block, pairs):
    return lax.ppermute(block, ("lat", "lon"), pairs)


def device(lat, lon):
    return lat * 16 + lon % 16


def exchange(net_in, coarse, tile_owner, lat):
    is_top, is_bottom = lat == 0, lat == 15
    first = net_in[:, :ROW_HALO].reshape(72, CH)
    last = net_in[:, ROWS - ROW_HALO :].reshape(72, CH)
    stored = coarse.reshape(12, CH)
    dest = lax.broadcasted_iota(jnp.int32, (16, 1, 1), 0)
    rows = jnp.where(
        dest == lat + 1, last[None], jnp.where(dest == lat - 1, first[None], jnp.zeros_like(first[None]))
    )
    sent = jnp.concatenate([rows, jnp.broadcast_to(stored[None], (16, 12, CH))], axis=1)
    got = lax.all_to_all(sent, "lat", 0, 0, tiled=True)
    above = jnp.maximum(lat - 1, 0)
    below = jnp.minimum(lat + 1, 15)

    def rows_from(i):
        return lax.dynamic_slice_in_dim(got, i, 1, 0)[0, :72].reshape(4, ROW_HALO, COLS)

    def coarse_from(i):
        return lax.dynamic_slice_in_dim(got, tile_owner[i], 1, 0)[0, 72:].reshape(12, 4, 32)

    own = coarse_from(lat)
    edge = jnp.where(is_bottom, own[:, 2:].reshape(6, CH), own[:, :2].reshape(6, CH))
    across = swap(
        jnp.concatenate([jnp.where(is_bottom, last, first), edge], axis=0),
        [(device(i, q), device(i, q + 8)) for i in range(16) for q in range(16)],
    )
    pole = across[:72].reshape(4, ROW_HALO, COLS)[:, ::-1]
    cpole = across[72:].reshape(12, 2, 32)[:, ::-1]
    north = jnp.where(is_top, pole, rows_from(above))
    south = jnp.where(is_bottom, pole, rows_from(below))
    cnorth = jnp.where(is_top, cpole, coarse_from(above)[:, 2:])
    csouth = jnp.where(is_bottom, cpole, coarse_from(below)[:, :2])
    tall = jnp.concatenate([north, net_in, south], axis=1)
    ctall = jnp.concatenate([cnorth, own, csouth], axis=1)

    def pack(fine, crs):
        crs = jnp.pad(crs.reshape(192), (0, 64)).reshape(2, CH)
        return jnp.concatenate([fine.reshape(25, CH), crs], axis=0)

    def unpack(block):
        fine = block[:25].reshape(4, EXT_ROWS, COL_HALO)
        return fine, block[25:].reshape(256)[:192].reshape(12, 8, 2)

    east = pack(tall[:, :, COLS - COL_HALO :], ctall[:, :, 30:])
    west = pack(tall[:, :, :COL_HALO], ctall[:, :, :2])
    odd = lax.axis_index("lon") % 2 == 1
    near = swap(
        jnp.where(odd, west, east),
        [(device(i, q), device(i, q ^ 1)) for i in range(16) for q in range(16)],
    )
    far = swap(
        jnp.where(odd, east, west),
        [(device(i, q), device(i, q + 1 if q % 2 else q - 1)) for i in range(16) for q in range(16)],
    )
    left, cleft = unpack(jnp.where(odd, near, far))
    right, cright = unpack(jnp.where(odd, far, near))
    wide = jnp.concatenate([left, tall, right], axis=2)
    cwide = jnp.concatenate([cleft, ctall, cright], axis=2)
    wide = jnp.pad(wide, ((0, 0), (0, 0), (0, LANES - EXT_COLS))).transpose(1, 0, 2)
    cwide = jnp.pad(cwide, ((0, 0), (0, 0), (EXT_COLS, LANES - EXT_COLS - COARSE_COLS))).transpose(1, 0, 2)
    cwide = jnp.repeat(cwide, RATIO, axis=0)[RATIO - 1 : RATIO - 1 + EXT_ROWS]
    return jnp.concatenate([wide, cwide], axis=1).reshape(EXT_ROWS * 16, LANES)


def body(
    current_sample,
    churn_noise,
    coarse_fields,
    tile_owner,
    input_kernel,
    fine_first,
    fine_second,
    coarse_first,
    coarse_second,
    output_kernel,
):
    lat = lax.axis_index("lat")
    scale_in = 1.0 / math.sqrt(DENOM)
    net_in = ((current_sample + CHURN * churn_noise) * scale_in).astype(BF)
    x = exchange(net_in, coarse_fields.astype(BF), tile_owner, lat)
    flags = jnp.stack([(lat == 0).astype(jnp.int32), (lat == 15).astype(jnp.int32)])
    return run_net(
        flags,
        x,
        current_sample,
        churn_noise,
        stem_weights(input_kernel),
        fine_first.reshape(9 * CH, CH),
        fine_second.reshape(9 * CH, CH),
        coarse_first.reshape(9 * CH, CH),
        coarse_second.reshape(9 * CH, CH),
        output_weights(output_kernel),
    )


def solution(mesh):
    placed = (P(None, "lat", "lon"),) * 3 + (P(),) * 7
    return jax.shard_map(
        body, mesh=mesh, in_specs=placed, out_specs=P(None, "lat", "lon"), check_vma=False
    )
```

```python
import math

import jax
import jax.numpy as jnp
from jax import lax
from jax.experimental import pallas as pl
from jax.experimental.pallas import tpu as pltpu
from jax.sharding import PartitionSpec as P


RATIO = 8
CH = 128
ROWS = 32
COLS = 256
ROW_HALO = 9
COL_HALO = 16
EXT_ROWS = ROWS + 2 * ROW_HALO
EXT_COLS = COLS + 2 * COL_HALO
COARSE_COLS = EXT_COLS // RATIO
LANES = 384
SEGS = 16
LEN = EXT_COLS // SEGS
CLEN = LEN // 2
GROUPS = 8
NF, NF2, NC = 4, 4, 5
N1, N2, N3 = 24 // NF, 22 // NF2, 10 // NC

sigma_now = 1.0
sigma_hat = 1.2
sigma_next = 0.4
sigma_data = 0.5
CHURN = math.sqrt(sigma_hat**2 - sigma_now**2)
DENOM = sigma_hat**2 + sigma_data**2
HALF = math.sqrt(0.5)
BF = jnp.bfloat16
F32 = jnp.float32


def silu(v):
    h = 0.5 * v
    return h + h * jnp.tanh(h)


def put_row(dst, row, val, n):
    dst[row, 1 : n + 1] = val.astype(BF)
    dst[row, 0] = pltpu.roll(val[n - 1], 1, 0).astype(BF)
    dst[row, n + 1] = pltpu.roll(val[0], SEGS - 1, 0).astype(BF)


def pair_rows(r, rows, top, bottom):
    mirrored = jnp.logical_or(
        jnp.logical_and(top == 1, r < 0), jnp.logical_and(bottom == 1, r >= rows)
    )
    return jnp.where(mirrored, r + 2, r - 1), jnp.where(mirrored, -1, 1)


def conv_pairs(src, firsts, w, n):
    lhs = jnp.concatenate(
        [
            jnp.concatenate(
                [
                    src[base + step * k, b : b + n].reshape(n * SEGS, CH)
                    for k in range(4)
                    for b in range(3)
                ],
                axis=1,
            )
            for base, step in firsts
        ],
        axis=0,
    )
    zero = jnp.zeros((3 * CH, CH), BF)
    rhs = jnp.concatenate(
        [jnp.concatenate([w[...], zero], 0), jnp.concatenate([zero, w[...]], 0)], 1
    )
    acc = jnp.dot(lhs, rhs, preferred_element_type=F32).reshape(len(firsts), n, SEGS, 2 * CH)
    return [(acc[i, :, :, :CH], acc[i, :, :, CH:]) for i in range(len(firsts))]


def net_kernel(
    flags,
    x,
    cur,
    noise,
    w_in_src,
    w_f1_src,
    w_f2_src,
    w_c1_src,
    w_c2_src,
    w_out_src,
    out,
    w_in,
    w_f1,
    w_f2,
    w_c1,
    w_c2,
    w_out,
    sems,
    a0,
    stem,
    act,
    hid,
    fine,
    pooled,
    cact,
    chid,
    merged,
    flat,
):
    top = flags[0]
    bottom = flags[1]
    copies = [
        pltpu.make_async_copy(src, dst, sems.at[n])
        for n, (src, dst) in enumerate(
            [
                (w_in_src, w_in),
                (w_f1_src, w_f1),
                (w_f2_src, w_f2),
                (w_c1_src, w_c1),
                (w_c2_src, w_c2),
                (w_out_src, w_out),
            ]
        )
    ]
    for copy in copies:
        copy.start()

    i = lax.broadcasted_iota(jnp.int32, ((LEN + 2) * SEGS, LANES), 0)
    lane = lax.broadcasted_iota(jnp.int32, ((LEN + 2) * SEGS, LANES), 1)
    col = LEN * (i & (SEGS - 1)) + (i >> 4) - 1
    inside = jnp.logical_and(col >= 0, col < EXT_COLS)
    hit = jnp.logical_or(lane == col, lane == EXT_COLS + (col >> 3))
    place = jnp.where(jnp.logical_and(inside, hit), 1.0, 0.0).astype(BF)
    for g in range(GROUPS):
        part = x[96 * g : 96 * g + 128, :]
        val = lax.dot_general(place, part, (((1,), (1,)), ((), ())), preferred_element_type=F32)
        a0[g] = val.reshape(LEN + 2, SEGS, CH).astype(BF)

    act[0] = jnp.zeros((LEN + 2, SEGS, CH), BF)
    act[EXT_ROWS - 1] = jnp.zeros((LEN + 2, SEGS, CH), BF)
    chid[0] = jnp.zeros((CLEN + 2, SEGS, CH), BF)
    chid[21] = jnp.zeros((CLEN + 2, SEGS, CH), BF)

    def stem_groups(groups, j, w):
        lhs = jnp.concatenate(
            [
                jnp.concatenate(
                    [a0[g, b : b + LEN].reshape(LEN * SEGS, CH) for b in range(3)], axis=1
                )
                for g in groups
            ],
            axis=0,
        )
        acc = jnp.dot(lhs, w, preferred_element_type=F32).reshape(len(groups), LEN, SEGS, 2 * CH)
        for n, g in enumerate(groups):
            r = 6 * g + 2 * j - 8
            for h in range(2):
                val = acc[n, :, :, h * CH : (h + 1) * CH].astype(BF)
                stem[r + 8 + h] = val
                put_row(act, r + 9 + h, silu(val.astype(F32)), LEN)

    copies[0].wait()
    for j in range(3):
        stem_groups([1, 2, 3, 4, 5, 6][j == 0 : 6 - (j == 2)], j, w_in[j])
        stem_groups([0, 1] if j == 0 else [0], j, w_in[3 * top + j])
        stem_groups([6, 7] if j == 2 else [7], j, w_in[3 * bottom + j])

    def first_body(p, carry):
        firsts = [pair_rows(2 * NF * p + 2 * i - 8, ROWS, top, bottom) for i in range(NF)]
        outs = conv_pairs(act, [(base + 9, step) for base, step in firsts], w_f1, LEN)
        for (base, step), (o0, o1) in zip(firsts, outs):
            put_row(hid, base + step + 8, silu(o0), LEN)
            put_row(hid, base + 2 * step + 8, silu(o1), LEN)
        return carry

    copies[1].wait()
    lax.fori_loop(0, N1, first_body, 0)

    def second_pairs(first, count):
        firsts = [pair_rows(2 * (first + i) - 6, ROWS, top, bottom) for i in range(count)]
        outs = conv_pairs(hid, [(base + 8, step) for base, step in firsts], w_f2, LEN)
        for i, ((base, step), (o0, o1)) in enumerate(zip(firsts, outs)):
            r0 = base + step
            r1 = base + 2 * step
            v0 = ((stem[r0 + 8].astype(F32) + o0) * HALF).astype(BF)
            v1 = ((stem[r1 + 8].astype(F32) + o1) * HALF).astype(BF)
            fine[r0 + 6] = v0
            fine[r1 + 6] = v1
            both = (v0.astype(F32) + v1.astype(F32)).reshape(CLEN, 2, SEGS, CH)
            mean = ((both[:, 0] + both[:, 1]) * 0.25).astype(BF)
            pooled[first + i] = mean
            put_row(cact, first + i, silu(mean.astype(F32)), CLEN)

    def second_body(p, carry):
        second_pairs(NF2 * p, NF2)
        return carry

    copies[2].wait()
    lax.fori_loop(0, N2, second_body, 0)
    second_pairs(NF2 * N2, 22 - NF2 * N2)

    def third_body(p, carry):
        firsts = [pair_rows(2 * NC * p + 2 * i - 2, ROWS // 2, top, bottom) for i in range(NC)]
        outs = conv_pairs(cact, [(base + 3, step) for base, step in firsts], w_c1, CLEN)
        for (base, step), (o0, o1) in zip(firsts, outs):
            put_row(chid, base + step + 3, silu(o0), CLEN)
            put_row(chid, base + 2 * step + 3, silu(o1), CLEN)
        return carry

    copies[3].wait()
    lax.fori_loop(0, N3, third_body, 0)

    def fourth_body(p, carry):
        firsts = [pair_rows(2 * NC * p + 2 * i - 2, ROWS // 2, top, bottom) for i in range(NC)]
        results = conv_pairs(chid, [(base + 3, step) for base, step in firsts], w_c2, CLEN)
        for (base, step), outs in zip(firsts, results):
            for h in range(2):
                cr = base + (h + 1) * step
                co = ((pooled[cr + 3].astype(F32) + outs[h]) * HALF).astype(BF).astype(F32)
                wide = jnp.broadcast_to(co[:, None], (CLEN, 2, SEGS, CH)).reshape(LEN, SEGS, CH)
                for q in range(2):
                    val = silu((fine[2 * cr + q + 6].astype(F32) + wide) * HALF)
                    put_row(merged, 2 * cr + q + 4, val, LEN)
        return carry

    copies[4].wait()
    lax.fori_loop(0, N3, fourth_body, 0)

    copies[5].wait()
    group_lane = lax.broadcasted_iota(jnp.int32, (LEN, SEGS, CH), 2) // 32
    rhs = jnp.concatenate([w_out[:, k * CH : (k + 1) * CH] for k in range(10)], axis=0)
    total = jnp.zeros((LEN, SEGS, CH), F32)
    for g in range(4):
        lhs = jnp.concatenate(
            [
                merged[8 * g + 3 + k].reshape((LEN + 2) * SEGS, CH)
                for k in range(10)
            ],
            axis=1,
        )
        z = jnp.dot(lhs, rhs, preferred_element_type=F32).reshape(LEN + 2, SEGS, CH)
        shift = 32 * g
        val = pltpu.roll(z[:LEN], shift, 2) if shift else z[:LEN]
        val = val + pltpu.roll(z[1 : LEN + 1], (96 + shift) % CH, 2)
        val = val + pltpu.roll(z[2:], (64 + shift) % CH, 2)
        total = jnp.where(group_lane == g, val, total)
    for l in range(LEN):
        flat[pl.ds(l, SEGS, stride=LEN), :] = total[l]
    rows = flat[COL_HALO : COL_HALO + COLS, :].T
    for g in range(4):
        for o in range(4):
            network = rows[32 * g + 8 * o : 32 * g + 8 * o + 8]
            at = pl.ds(8 * g, 8)
            perturbed = cur[o, at] + CHURN * noise[o, at]
            denoised = (
                sigma_data**2 / DENOM * perturbed
                + sigma_hat * sigma_data / math.sqrt(DENOM) * network
            )
            out[o, at] = perturbed + (sigma_next - sigma_hat) / sigma_hat * (perturbed - denoised)


def run_net(flags, x, cur, noise, w_in, w_f1, w_f2, w_c1, w_c2, w_out):
    vmem = pl.BlockSpec(memory_space=pltpu.VMEM)
    row = (LEN + 2, SEGS, CH)
    crow = (CLEN + 2, SEGS, CH)
    return pl.pallas_call(
        net_kernel,
        out_shape=jax.ShapeDtypeStruct((4, ROWS, COLS), F32),
        in_specs=[pl.BlockSpec(memory_space=pltpu.SMEM)]
        + [vmem] * 3
        + [pl.BlockSpec(memory_space=pl.ANY)] * 6,
        out_specs=vmem,
        scratch_shapes=[
            pltpu.VMEM((6, 3 * CH, 2 * CH), BF),
            pltpu.VMEM((9 * CH, CH), BF),
            pltpu.VMEM((9 * CH, CH), BF),
            pltpu.VMEM((9 * CH, CH), BF),
            pltpu.VMEM((9 * CH, CH), BF),
            pltpu.VMEM((CH, 10 * CH), BF),
            pltpu.SemaphoreType.DMA((6,)),
            pltpu.VMEM((GROUPS,) + row, BF),
            pltpu.VMEM((48, LEN, SEGS, CH), BF),
            pltpu.VMEM((EXT_ROWS,) + row, BF),
            pltpu.VMEM((48,) + row, BF),
            pltpu.VMEM((44, LEN, SEGS, CH), BF),
            pltpu.VMEM((22, CLEN, SEGS, CH), BF),
            pltpu.VMEM((22,) + crow, BF),
            pltpu.VMEM((22,) + crow, BF),
            pltpu.VMEM((40,) + row, BF),
            pltpu.VMEM((EXT_COLS, CH), F32),
        ],
        compiler_params=pltpu.CompilerParams(vmem_limit_bytes=58 * 1024 * 1024),
        name="net",
    )(flags, x, cur, noise, w_in, w_f1, w_f2, w_c1, w_c2, w_out)


def stem_weights(kernel):
    tables = []
    for k in (kernel, kernel[::-1]):
        k = k.transpose(1, 0, 2, 3)
        for j in range(3):
            first = jnp.pad(k, ((0, 0), (2 * j, 5 - 2 * j), (0, 0), (0, 0)))
            second = jnp.pad(k, ((0, 0), (2 * j + 1, 4 - 2 * j), (0, 0), (0, 0)))
            tables.append(jnp.concatenate([first, second], axis=3).reshape(3 * 8 * 16, 2 * CH))
    return jnp.stack(tables)


def output_weights(kernel):
    per_row = []
    for r in range(8):
        per_row.append(jnp.pad(kernel, ((r, 7 - r), (0, 0), (0, 0), (0, 0))))
    w = jnp.stack(per_row)
    w = w.transpose(3, 1, 2, 4, 0).reshape(CH, 10, 96)
    return jnp.pad(w, ((0, 0), (0, 0), (0, 32))).reshape(CH, 10 * CH)


def swap(block, pairs):
    return lax.ppermute(block, ("lat", "lon"), pairs)


def device(lat, lon):
    return lat * 16 + lon % 16


def exchange(net_in, coarse, tile_owner, lat):
    is_top, is_bottom = lat == 0, lat == 15
    first = net_in[:, :ROW_HALO].reshape(72, CH)
    last = net_in[:, ROWS - ROW_HALO :].reshape(72, CH)
    stored = coarse.reshape(12, CH)
    dest = lax.broadcasted_iota(jnp.int32, (16, 1, 1), 0)
    rows = jnp.where(
        dest == lat + 1, last[None], jnp.where(dest == lat - 1, first[None], jnp.zeros_like(first[None]))
    )
    sent = jnp.concatenate([rows, jnp.broadcast_to(stored[None], (16, 12, CH))], axis=1)
    got = lax.all_to_all(sent, "lat", 0, 0, tiled=True)
    above = jnp.maximum(lat - 1, 0)
    below = jnp.minimum(lat + 1, 15)

    def rows_from(i):
        return lax.dynamic_slice_in_dim(got, i, 1, 0)[0, :72].reshape(4, ROW_HALO, COLS)

    def coarse_from(i):
        return lax.dynamic_slice_in_dim(got, tile_owner[i], 1, 0)[0, 72:].reshape(12, 4, 32)

    own = coarse_from(lat)
    edge = jnp.where(is_bottom, own[:, 2:].reshape(6, CH), own[:, :2].reshape(6, CH))
    across = swap(
        jnp.concatenate([jnp.where(is_bottom, last, first), edge], axis=0),
        [(device(i, q), device(i, q + 8)) for i in range(16) for q in range(16)],
    )
    pole = across[:72].reshape(4, ROW_HALO, COLS)[:, ::-1]
    cpole = across[72:].reshape(12, 2, 32)[:, ::-1]
    north = jnp.where(is_top, pole, rows_from(above))
    south = jnp.where(is_bottom, pole, rows_from(below))
    cnorth = jnp.where(is_top, cpole, coarse_from(above)[:, 2:])
    csouth = jnp.where(is_bottom, cpole, coarse_from(below)[:, :2])
    tall = jnp.concatenate([north, net_in, south], axis=1)
    ctall = jnp.concatenate([cnorth, own, csouth], axis=1)

    def pack(fine, crs):
        crs = jnp.pad(crs.reshape(192), (0, 64)).reshape(2, CH)
        return jnp.concatenate([fine.reshape(25, CH), crs], axis=0)

    def unpack(block):
        fine = block[:25].reshape(4, EXT_ROWS, COL_HALO)
        return fine, block[25:].reshape(256)[:192].reshape(12, 8, 2)

    east = pack(tall[:, :, COLS - COL_HALO :], ctall[:, :, 30:])
    west = pack(tall[:, :, :COL_HALO], ctall[:, :, :2])
    odd = lax.axis_index("lon") % 2 == 1
    near = swap(
        jnp.where(odd, west, east),
        [(device(i, q), device(i, q ^ 1)) for i in range(16) for q in range(16)],
    )
    far = swap(
        jnp.where(odd, east, west),
        [(device(i, q), device(i, q + 1 if q % 2 else q - 1)) for i in range(16) for q in range(16)],
    )
    left, cleft = unpack(jnp.where(odd, near, far))
    right, cright = unpack(jnp.where(odd, far, near))
    wide = jnp.concatenate([left, tall, right], axis=2)
    cwide = jnp.concatenate([cleft, ctall, cright], axis=2)
    wide = jnp.pad(wide, ((0, 0), (0, 0), (0, LANES - EXT_COLS))).transpose(1, 0, 2)
    cwide = jnp.pad(cwide, ((0, 0), (0, 0), (EXT_COLS, LANES - EXT_COLS - COARSE_COLS))).transpose(1, 0, 2)
    cwide = jnp.repeat(cwide, RATIO, axis=0)[RATIO - 1 : RATIO - 1 + EXT_ROWS]
    return jnp.concatenate([wide, cwide], axis=1).reshape(EXT_ROWS * 16, LANES)


def body(
    current_sample,
    churn_noise,
    coarse_fields,
    tile_owner,
    input_kernel,
    fine_first,
    fine_second,
    coarse_first,
    coarse_second,
    output_kernel,
):
    lat = lax.axis_index("lat")
    scale_in = 1.0 / math.sqrt(DENOM)
    net_in = ((current_sample + CHURN * churn_noise) * scale_in).astype(BF)
    x = exchange(net_in, coarse_fields.astype(BF), tile_owner, lat)
    flags = jnp.stack([(lat == 0).astype(jnp.int32), (lat == 15).astype(jnp.int32)])
    return run_net(
        flags,
        x,
        current_sample,
        churn_noise,
        stem_weights(input_kernel),
        fine_first.reshape(9 * CH, CH),
        fine_second.reshape(9 * CH, CH),
        coarse_first.reshape(9 * CH, CH),
        coarse_second.reshape(9 * CH, CH),
        output_weights(output_kernel),
    )


def solution(mesh):
    placed = (P(None, "lat", "lon"),) * 3 + (P(),) * 7
    return jax.shard_map(
        body, mesh=mesh, in_specs=placed, out_specs=P(None, "lat", "lon"), check_vma=False
    )
```

```python
import math

import jax
import jax.numpy as jnp
from jax import lax
from jax.experimental import pallas as pl
from jax.experimental.pallas import tpu as pltpu
from jax.sharding import PartitionSpec as P


RATIO = 8
CH = 128
ROWS = 32
COLS = 256
ROW_HALO = 9
COL_HALO = 16
EXT_ROWS = ROWS + 2 * ROW_HALO
EXT_COLS = COLS + 2 * COL_HALO
COARSE_COLS = EXT_COLS // RATIO
LANES = 384
SEGS = 16
LEN = EXT_COLS // SEGS
CLEN = LEN // 2
GROUPS = 8
NF, NF2, NC = 6, 6, 5
N1, N2, N3 = 24 // NF, 22 // NF2, 10 // NC

sigma_now = 1.0
sigma_hat = 1.2
sigma_next = 0.4
sigma_data = 0.5
CHURN = math.sqrt(sigma_hat**2 - sigma_now**2)
DENOM = sigma_hat**2 + sigma_data**2
HALF = math.sqrt(0.5)
BF = jnp.bfloat16
F32 = jnp.float32


def silu(v):
    h = 0.5 * v
    return h + h * jnp.tanh(h)


def put_row(dst, row, val, n):
    dst[row, 1 : n + 1] = val.astype(BF)
    dst[row, 0] = pltpu.roll(val[n - 1], 1, 0).astype(BF)
    dst[row, n + 1] = pltpu.roll(val[0], SEGS - 1, 0).astype(BF)


def pair_rows(r, rows, top, bottom):
    mirrored = jnp.logical_or(
        jnp.logical_and(top == 1, r < 0), jnp.logical_and(bottom == 1, r >= rows)
    )
    return jnp.where(mirrored, r + 2, r - 1), jnp.where(mirrored, -1, 1)


def conv_pairs(src, firsts, w, n):
    lhs = jnp.concatenate(
        [
            jnp.concatenate(
                [
                    src[base + step * k, b : b + n].reshape(n * SEGS, CH)
                    for k in range(4)
                    for b in range(3)
                ],
                axis=1,
            )
            for base, step in firsts
        ],
        axis=0,
    )
    zero = jnp.zeros((3 * CH, CH), BF)
    rhs = jnp.concatenate(
        [jnp.concatenate([w[...], zero], 0), jnp.concatenate([zero, w[...]], 0)], 1
    )
    acc = jnp.dot(lhs, rhs, preferred_element_type=F32).reshape(len(firsts), n, SEGS, 2 * CH)
    return [(acc[i, :, :, :CH], acc[i, :, :, CH:]) for i in range(len(firsts))]


def fine_pairs(src, firsts, w):
    n = LEN
    zero = jnp.zeros((CH, CH), BF)

    def tap(a, b):
        return w[(3 * a + b) * CH : (3 * a + b + 1) * CH, :]

    lhs = jnp.concatenate(
        [
            jnp.concatenate(
                [
                    src[base + step * k, b : b + n].reshape(n * SEGS, CH)
                    for k in (1, 2)
                    for b in range(3)
                ],
                axis=1,
            )
            for base, step in firsts
        ],
        axis=0,
    )
    rhs = jnp.concatenate([w[3 * CH :, :], w[: 6 * CH, :]], axis=0)
    rhs = jnp.concatenate([rhs[: 6 * CH], rhs[6 * CH :]], axis=1)
    inner = jnp.dot(lhs, rhs, preferred_element_type=F32).reshape(len(firsts), n, SEGS, 2 * CH)
    outer = []
    for k, a in ((0, 0), (3, 2)):
        parts = []
        for base, step in firsts:
            row = src[base + step * k].reshape(CLEN + 1, 2, SEGS, CH)
            cols = [row[i : i + CLEN, j].reshape(CLEN * SEGS, CH) for i in range(2) for j in range(2)]
            parts.append(jnp.concatenate(cols, axis=1))
        even = jnp.concatenate([tap(a, 0), tap(a, 1), tap(a, 2), zero], axis=0)
        odd = jnp.concatenate([zero, tap(a, 0), tap(a, 1), tap(a, 2)], axis=0)
        got = jnp.dot(
            jnp.concatenate(parts, axis=0),
            jnp.concatenate([even, odd], axis=1),
            preferred_element_type=F32,
        ).reshape(len(firsts), CLEN, SEGS, 2 * CH)
        outer.append(jnp.stack([got[..., :CH], got[..., CH:]], axis=2).reshape(len(firsts), n, SEGS, CH))
    return [
        (inner[i, :, :, :CH] + outer[0][i], inner[i, :, :, CH:] + outer[1][i])
        for i in range(len(firsts))
    ]


def net_kernel(
    flags,
    x,
    cur,
    noise,
    w_in_src,
    w_f1_src,
    w_f2_src,
    w_c1_src,
    w_c2_src,
    w_out_src,
    out,
    w_in,
    w_f1,
    w_f2,
    w_c1,
    w_c2,
    w_out,
    sems,
    a0,
    stem,
    act,
    hid,
    fine,
    pooled,
    cact,
    chid,
    merged,
    flat,
):
    top = flags[0]
    bottom = flags[1]
    copies = [
        pltpu.make_async_copy(src, dst, sems.at[n])
        for n, (src, dst) in enumerate(
            [
                (w_in_src, w_in),
                (w_f1_src, w_f1),
                (w_f2_src, w_f2),
                (w_c1_src, w_c1),
                (w_c2_src, w_c2),
                (w_out_src, w_out),
            ]
        )
    ]
    for copy in copies:
        copy.start()

    i = lax.broadcasted_iota(jnp.int32, ((LEN + 2) * SEGS, LANES), 0)
    lane = lax.broadcasted_iota(jnp.int32, ((LEN + 2) * SEGS, LANES), 1)
    col = LEN * (i & (SEGS - 1)) + (i >> 4) - 1
    inside = jnp.logical_and(col >= 0, col < EXT_COLS)
    hit = jnp.logical_or(lane == col, lane == EXT_COLS + (col >> 3))
    place = jnp.where(jnp.logical_and(inside, hit), 1.0, 0.0).astype(BF)
    for g in range(GROUPS):
        part = x[96 * g : 96 * g + 128, :]
        val = lax.dot_general(place, part, (((1,), (1,)), ((), ())), preferred_element_type=F32)
        a0[g] = val.reshape(LEN + 2, SEGS, CH).astype(BF)

    act[0] = jnp.zeros((LEN + 2, SEGS, CH), BF)
    act[EXT_ROWS - 1] = jnp.zeros((LEN + 2, SEGS, CH), BF)
    chid[0] = jnp.zeros((CLEN + 2, SEGS, CH), BF)
    chid[21] = jnp.zeros((CLEN + 2, SEGS, CH), BF)

    def stem_groups(groups, j, w):
        lhs = jnp.concatenate(
            [
                jnp.concatenate(
                    [a0[g, b : b + LEN].reshape(LEN * SEGS, CH) for b in range(3)], axis=1
                )
                for g in groups
            ],
            axis=0,
        )
        acc = jnp.dot(lhs, w, preferred_element_type=F32).reshape(len(groups), LEN, SEGS, 2 * CH)
        for n, g in enumerate(groups):
            r = 6 * g + 2 * j - 8
            for h in range(2):
                val = acc[n, :, :, h * CH : (h + 1) * CH].astype(BF)
                stem[r + 8 + h] = val
                put_row(act, r + 9 + h, silu(val.astype(F32)), LEN)

    copies[0].wait()
    for j in range(3):
        stem_groups([1, 2, 3, 4, 5, 6][j == 0 : 6 - (j == 2)], j, w_in[j])
        stem_groups([0, 1] if j == 0 else [0], j, w_in[3 * top + j])
        stem_groups([6, 7] if j == 2 else [7], j, w_in[3 * bottom + j])

    def first_body(p, carry):
        firsts = [pair_rows(2 * NF * p + 2 * i - 8, ROWS, top, bottom) for i in range(NF)]
        outs = fine_pairs(act, [(base + 9, step) for base, step in firsts], w_f1)
        for (base, step), (o0, o1) in zip(firsts, outs):
            put_row(hid, base + step + 8, silu(o0), LEN)
            put_row(hid, base + 2 * step + 8, silu(o1), LEN)
        return carry

    copies[1].wait()
    lax.fori_loop(0, N1, first_body, 0)

    def second_pairs(first, count):
        firsts = [pair_rows(2 * (first + i) - 6, ROWS, top, bottom) for i in range(count)]
        outs = fine_pairs(hid, [(base + 8, step) for base, step in firsts], w_f2)
        for i, ((base, step), (o0, o1)) in enumerate(zip(firsts, outs)):
            r0 = base + step
            r1 = base + 2 * step
            v0 = ((stem[r0 + 8].astype(F32) + o0) * HALF).astype(BF)
            v1 = ((stem[r1 + 8].astype(F32) + o1) * HALF).astype(BF)
            fine[r0 + 6] = v0
            fine[r1 + 6] = v1
            both = (v0.astype(F32) + v1.astype(F32)).reshape(CLEN, 2, SEGS, CH)
            mean = ((both[:, 0] + both[:, 1]) * 0.25).astype(BF)
            pooled[first + i] = mean
            put_row(cact, first + i, silu(mean.astype(F32)), CLEN)

    def second_body(p, carry):
        second_pairs(NF2 * p, NF2)
        return carry

    copies[2].wait()
    lax.fori_loop(0, N2, second_body, 0)
    second_pairs(NF2 * N2, 22 - NF2 * N2)

    def third_body(p, carry):
        firsts = [pair_rows(2 * NC * p + 2 * i - 2, ROWS // 2, top, bottom) for i in range(NC)]
        outs = conv_pairs(cact, [(base + 3, step) for base, step in firsts], w_c1, CLEN)
        for (base, step), (o0, o1) in zip(firsts, outs):
            put_row(chid, base + step + 3, silu(o0), CLEN)
            put_row(chid, base + 2 * step + 3, silu(o1), CLEN)
        return carry

    copies[3].wait()
    lax.fori_loop(0, N3, third_body, 0)

    def fourth_body(p, carry):
        firsts = [pair_rows(2 * NC * p + 2 * i - 2, ROWS // 2, top, bottom) for i in range(NC)]
        results = conv_pairs(chid, [(base + 3, step) for base, step in firsts], w_c2, CLEN)
        for (base, step), outs in zip(firsts, results):
            for h in range(2):
                cr = base + (h + 1) * step
                co = ((pooled[cr + 3].astype(F32) + outs[h]) * HALF).astype(BF).astype(F32)
                wide = jnp.broadcast_to(co[:, None], (CLEN, 2, SEGS, CH)).reshape(LEN, SEGS, CH)
                for q in range(2):
                    val = silu((fine[2 * cr + q + 6].astype(F32) + wide) * HALF)
                    put_row(merged, 2 * cr + q + 4, val, LEN)
        return carry

    copies[4].wait()
    lax.fori_loop(0, N3, fourth_body, 0)

    copies[5].wait()
    group_lane = lax.broadcasted_iota(jnp.int32, (LEN, SEGS, CH), 2) // 32
    rhs = jnp.concatenate([w_out[:, k * CH : (k + 1) * CH] for k in range(10)], axis=0)
    total = jnp.zeros((LEN, SEGS, CH), F32)
    for g in range(4):
        lhs = jnp.concatenate(
            [
                merged[8 * g + 3 + k].reshape((LEN + 2) * SEGS, CH)
                for k in range(10)
            ],
            axis=1,
        )
        z = jnp.dot(lhs, rhs, preferred_element_type=F32).reshape(LEN + 2, SEGS, CH)
        shift = 32 * g
        val = pltpu.roll(z[:LEN], shift, 2) if shift else z[:LEN]
        val = val + pltpu.roll(z[1 : LEN + 1], (96 + shift) % CH, 2)
        val = val + pltpu.roll(z[2:], (64 + shift) % CH, 2)
        total = jnp.where(group_lane == g, val, total)
    for l in range(LEN):
        flat[pl.ds(l, SEGS, stride=LEN), :] = total[l]
    rows = flat[COL_HALO : COL_HALO + COLS, :].T
    for g in range(4):
        for o in range(4):
            network = rows[32 * g + 8 * o : 32 * g + 8 * o + 8]
            at = pl.ds(8 * g, 8)
            perturbed = cur[o, at] + CHURN * noise[o, at]
            denoised = (
                sigma_data**2 / DENOM * perturbed
                + sigma_hat * sigma_data / math.sqrt(DENOM) * network
            )
            out[o, at] = perturbed + (sigma_next - sigma_hat) / sigma_hat * (perturbed - denoised)


def run_net(flags, x, cur, noise, w_in, w_f1, w_f2, w_c1, w_c2, w_out):
    vmem = pl.BlockSpec(memory_space=pltpu.VMEM)
    row = (LEN + 2, SEGS, CH)
    crow = (CLEN + 2, SEGS, CH)
    return pl.pallas_call(
        net_kernel,
        out_shape=jax.ShapeDtypeStruct((4, ROWS, COLS), F32),
        in_specs=[pl.BlockSpec(memory_space=pltpu.SMEM)]
        + [vmem] * 3
        + [pl.BlockSpec(memory_space=pl.ANY)] * 6,
        out_specs=vmem,
        scratch_shapes=[
            pltpu.VMEM((6, 3 * CH, 2 * CH), BF),
            pltpu.VMEM((9 * CH, CH), BF),
            pltpu.VMEM((9 * CH, CH), BF),
            pltpu.VMEM((9 * CH, CH), BF),
            pltpu.VMEM((9 * CH, CH), BF),
            pltpu.VMEM((CH, 10 * CH), BF),
            pltpu.SemaphoreType.DMA((6,)),
            pltpu.VMEM((GROUPS,) + row, BF),
            pltpu.VMEM((48, LEN, SEGS, CH), BF),
            pltpu.VMEM((EXT_ROWS,) + row, BF),
            pltpu.VMEM((48,) + row, BF),
            pltpu.VMEM((44, LEN, SEGS, CH), BF),
            pltpu.VMEM((22, CLEN, SEGS, CH), BF),
            pltpu.VMEM((22,) + crow, BF),
            pltpu.VMEM((22,) + crow, BF),
            pltpu.VMEM((40,) + row, BF),
            pltpu.VMEM((EXT_COLS, CH), F32),
        ],
        compiler_params=pltpu.CompilerParams(vmem_limit_bytes=58 * 1024 * 1024),
        name="net",
    )(flags, x, cur, noise, w_in, w_f1, w_f2, w_c1, w_c2, w_out)


def stem_weights(kernel):
    tables = []
    for k in (kernel, kernel[::-1]):
        k = k.transpose(1, 0, 2, 3)
        for j in range(3):
            first = jnp.pad(k, ((0, 0), (2 * j, 5 - 2 * j), (0, 0), (0, 0)))
            second = jnp.pad(k, ((0, 0), (2 * j + 1, 4 - 2 * j), (0, 0), (0, 0)))
            tables.append(jnp.concatenate([first, second], axis=3).reshape(3 * 8 * 16, 2 * CH))
    return jnp.stack(tables)


def output_weights(kernel):
    per_row = []
    for r in range(8):
        per_row.append(jnp.pad(kernel, ((r, 7 - r), (0, 0), (0, 0), (0, 0))))
    w = jnp.stack(per_row)
    w = w.transpose(3, 1, 2, 4, 0).reshape(CH, 10, 96)
    return jnp.pad(w, ((0, 0), (0, 0), (0, 32))).reshape(CH, 10 * CH)


def swap(block, pairs):
    return lax.ppermute(block, ("lat", "lon"), pairs)


def device(lat, lon):
    return lat * 16 + lon % 16


def exchange(net_in, coarse, tile_owner, lat):
    is_top, is_bottom = lat == 0, lat == 15
    first = net_in[:, :ROW_HALO].reshape(72, CH)
    last = net_in[:, ROWS - ROW_HALO :].reshape(72, CH)
    stored = coarse.reshape(12, CH)
    dest = lax.broadcasted_iota(jnp.int32, (16, 1, 1), 0)
    rows = jnp.where(
        dest == lat + 1, last[None], jnp.where(dest == lat - 1, first[None], jnp.zeros_like(first[None]))
    )
    sent = jnp.concatenate([rows, jnp.broadcast_to(stored[None], (16, 12, CH))], axis=1)
    got = lax.all_to_all(sent, "lat", 0, 0, tiled=True)
    above = jnp.maximum(lat - 1, 0)
    below = jnp.minimum(lat + 1, 15)

    def rows_from(i):
        return lax.dynamic_slice_in_dim(got, i, 1, 0)[0, :72].reshape(4, ROW_HALO, COLS)

    def coarse_from(i):
        return lax.dynamic_slice_in_dim(got, tile_owner[i], 1, 0)[0, 72:].reshape(12, 4, 32)

    own = coarse_from(lat)
    edge = jnp.where(is_bottom, own[:, 2:].reshape(6, CH), own[:, :2].reshape(6, CH))
    across = swap(
        jnp.concatenate([jnp.where(is_bottom, last, first), edge], axis=0),
        [(device(i, q), device(i, q + 8)) for i in range(16) for q in range(16)],
    )
    pole = across[:72].reshape(4, ROW_HALO, COLS)[:, ::-1]
    cpole = across[72:].reshape(12, 2, 32)[:, ::-1]
    north = jnp.where(is_top, pole, rows_from(above))
    south = jnp.where(is_bottom, pole, rows_from(below))
    cnorth = jnp.where(is_top, cpole, coarse_from(above)[:, 2:])
    csouth = jnp.where(is_bottom, cpole, coarse_from(below)[:, :2])
    tall = jnp.concatenate([north, net_in, south], axis=1)
    ctall = jnp.concatenate([cnorth, own, csouth], axis=1)

    def pack(fine, crs):
        crs = jnp.pad(crs.reshape(192), (0, 64)).reshape(2, CH)
        return jnp.concatenate([fine.reshape(25, CH), crs], axis=0)

    def unpack(block):
        fine = block[:25].reshape(4, EXT_ROWS, COL_HALO)
        return fine, block[25:].reshape(256)[:192].reshape(12, 8, 2)

    east = pack(tall[:, :, COLS - COL_HALO :], ctall[:, :, 30:])
    west = pack(tall[:, :, :COL_HALO], ctall[:, :, :2])
    odd = lax.axis_index("lon") % 2 == 1
    near = swap(
        jnp.where(odd, west, east),
        [(device(i, q), device(i, q ^ 1)) for i in range(16) for q in range(16)],
    )
    far = swap(
        jnp.where(odd, east, west),
        [(device(i, q), device(i, q + 1 if q % 2 else q - 1)) for i in range(16) for q in range(16)],
    )
    left, cleft = unpack(jnp.where(odd, near, far))
    right, cright = unpack(jnp.where(odd, far, near))
    wide = jnp.concatenate([left, tall, right], axis=2)
    cwide = jnp.concatenate([cleft, ctall, cright], axis=2)
    wide = jnp.pad(wide, ((0, 0), (0, 0), (0, LANES - EXT_COLS))).transpose(1, 0, 2)
    cwide = jnp.pad(cwide, ((0, 0), (0, 0), (EXT_COLS, LANES - EXT_COLS - COARSE_COLS))).transpose(1, 0, 2)
    cwide = jnp.repeat(cwide, RATIO, axis=0)[RATIO - 1 : RATIO - 1 + EXT_ROWS]
    return jnp.concatenate([wide, cwide], axis=1).reshape(EXT_ROWS * 16, LANES)


def body(
    current_sample,
    churn_noise,
    coarse_fields,
    tile_owner,
    input_kernel,
    fine_first,
    fine_second,
    coarse_first,
    coarse_second,
    output_kernel,
):
    lat = lax.axis_index("lat")
    scale_in = 1.0 / math.sqrt(DENOM)
    net_in = ((current_sample + CHURN * churn_noise) * scale_in).astype(BF)
    x = exchange(net_in, coarse_fields.astype(BF), tile_owner, lat)
    flags = jnp.stack([(lat == 0).astype(jnp.int32), (lat == 15).astype(jnp.int32)])
    return run_net(
        flags,
        x,
        current_sample,
        churn_noise,
        stem_weights(input_kernel),
        fine_first.reshape(9 * CH, CH),
        fine_second.reshape(9 * CH, CH),
        coarse_first.reshape(9 * CH, CH),
        coarse_second.reshape(9 * CH, CH),
        output_weights(output_kernel),
    )


def solution(mesh):
    placed = (P(None, "lat", "lon"),) * 3 + (P(),) * 7
    return jax.shard_map(
        body, mesh=mesh, in_specs=placed, out_specs=P(None, "lat", "lon"), check_vma=False
    )
```
